128 devices in a mesh: ctx: 16 (over y, x), tp: 8 (over z, core).
Axes of the slice: x: 4, y: 4, z: 4, core: 2. Of those that a mesh axis runs over, the one named last changes fastest.
Arguments:
- qkv_first: bfloat16 [3, 16384, 4096], P(None, 'ctx', 'tp'), may hold values from -6 to 6
- short_first: float32 [3, 3, 4096], P(None, None, 'tp'), may hold values from -4 to 4
- medium_filter: bfloat16 [4096, 128], P('tp'), may hold values from -0.5 to 0.5
- out_weight: bfloat16 [4096, 4096], P('tp', 'ctx'), may hold values from -0.09375 to 0.09375
- residual_in: bfloat16 [16384, 4096], P('ctx', 'tp'), may hold values from -64 to 64
- norm_gain: bfloat16 [4096], P('tp'), may hold values from 0.5 to 1.5
- in_weight: bfloat16 [3, 4096, 4096], P(None, 'ctx', 'tp'), may hold values from -0.09375 to 0.09375
- short_second: float32 [3, 3, 4096], P(None, None, 'tp'), may hold values from -4 to 4
- rates: float32 [16, 4096], P(None, 'tp'), as said below
- residues: float32 [16, 4096], P(None, 'tp'), may hold values from -0.024 to 0.024
- skip_gain: float32 [4096], P('tp'), may hold values from -4 to 4
Outputs:
- hidden: bfloat16 [16384, 4096], P('ctx', 'tp')
- mixed: bfloat16 [16384, 4096], P('ctx', 'tp')
The draws below stay inside these ranges and needn't reach their ends.
Inputs may be any that keep to these rules, and one draw needn't show every extreme that they name: `rates`: each entry is a positive decay rate per token, between 1e-7 and 0.05.
All inputs are finite; a program needn't handle non-finite values.
Results may differ from the reference program's by a relative error of at most 0.025.
Values may be sent and summed in bfloat16 or wider, within the bound.
No kernel may reach another device: no remote copies, remote signals or barrier semaphores. Data moves between devices by JAX's collectives and lax.ppermute only.
A program may use at most 128 MiB of HBM per device.

```python
import math
import jax
import jax.numpy as jnp
from jax import lax

D = 4096
POLES = 16
TAPS = 128
SHORT = 3
TOKENS = 16384
N_TP = 8


def draw_residual_in(key, part):
    row_key = jax.random.fold_in(key, 11)
    entry_key = jax.random.fold_in(key, 12)
    columns = jnp.arange(D, dtype=jnp.float32) / D
    column_scale = 10.0 ** (columns - 0.5)
    row_scale = jnp.exp(jax.random.uniform(row_key, (TOKENS, 1), jnp.float32, math.log(0.3), math.log(3.0)))
    values = jnp.clip(jax.random.normal(entry_key, (TOKENS, D), jnp.float32), -6.0, 6.0)
    return (values * row_scale * column_scale[None, :]).astype(jnp.bfloat16)


def draw_rates(key, part):
    level_key = jax.random.fold_in(key, 22)
    levels = jax.random.uniform(level_key, (POLES, D), jnp.float32)
    lower_log = math.log(1e-07)
    upper_log = jnp.full((POLES, D), math.log(0.05), jnp.float32)
    return jnp.exp(lower_log + levels * (upper_log - lower_log)).astype(jnp.float32)


def block_levels(rng, dims, cuts, low, top_value):
    loudness = 1.0
    for dim, blocks in cuts:
        steps = jax.random.uniform(jax.random.fold_in(jax.random.fold_in(rng, 6), dim), (blocks,), jnp.float32, low / len(cuts), top_value / len(cuts))
        loudness = loudness * jnp.repeat(jnp.exp(steps), dims[dim] // blocks).reshape((-1,) + (1,) * (len(dims) - 1 - dim))
    return loudness


def gaussian(key, dims, deviation, most, cuts=(), held_as=jnp.bfloat16):
    factor_of = block_levels(key, dims, cuts, -0.22, 0.18) if cuts else 1.0
    array = jax.random.normal(key, dims, jnp.float32) * deviation * factor_of
    return jnp.minimum(jnp.maximum(array, -most), most).astype(held_as)


def setup_inputs(seed: int = 0) -> dict:
    arg_keys = jax.random.split(jax.random.key(seed), 12)
    return {
        "qkv_first": gaussian(arg_keys[0], (3, TOKENS, D), 1.0, 6.0, ((1, 16), (2, 8))),
        "short_first": gaussian(arg_keys[1], (3, SHORT, D), 0.6, 4.0, ((2, 8),), jnp.float32),
        "medium_filter": gaussian(arg_keys[2], (D, TAPS), TAPS ** -0.5, 0.5, ((0, 8),)),
        "out_weight": gaussian(arg_keys[3], (D, D), D ** -0.5, 0.09375, ((0, 8), (1, 16))),
        "residual_in": draw_residual_in(jax.random.fold_in(arg_keys[11], 71), 0),
        "norm_gain": jnp.clip(1.0 + 0.1 * jax.random.normal(arg_keys[5], (D,), jnp.float32), 0.5, 1.5).astype(jnp.bfloat16),
        "in_weight": gaussian(arg_keys[6], (3, D, D), D ** -0.5, 0.09375, ((1, 16), (2, 8))),
        "short_second": gaussian(arg_keys[7], (3, SHORT, D), 0.6, 4.0, ((2, 8),), jnp.float32),
        "rates": draw_rates(jax.random.fold_in(arg_keys[11], 71), 0),
        "residues": gaussian(arg_keys[9], (POLES, D), 0.004, 0.024, ((1, 8),), jnp.float32),
        "skip_gain": gaussian(arg_keys[10], (D,), 1.0, 4.0, ((0, 8),), jnp.float32),
    }


EPSILON = 1e-05

def featurize(extended, tap_weights):
    widened = extended.astype(jnp.float32)
    return tap_weights[:, 0][:, None, :] * widened[:, 2:] + tap_weights[:, 1][:, None, :] * widened[:, 1:-1] + tap_weights[:, 2][:, None, :] * widened[:, :-2]

def medium_reference(gated, filters):
    length = gated.shape[0]
    padded = jnp.pad(gated.astype(jnp.float32), ((TAPS - 1, 0), (0, 0)))
    filter_values = filters.astype(jnp.float32)

    def add_tap(lag_index, totals):
        shifted = lax.dynamic_slice_in_dim(padded, (TAPS - 1 - lag_index).astype(jnp.int32), length, 0)
        column = lax.dynamic_slice_in_dim(filter_values, lag_index.astype(jnp.int32), 1, 1)[:, 0]
        return totals + shifted * column
    return lax.fori_loop(0, TAPS, add_tap, jnp.zeros(gated.shape, jnp.float32))

def modal_reference(gated, rates, residues):
    inputs = gated.astype(jnp.float32)
    poles = jnp.exp(-rates)

    def advance(state, row_input):
        state = poles * state + row_input[None, :]
        return (state, lax.optimization_barrier(jnp.sum(residues * state, axis=0)))
    _, outputs = lax.scan(advance, jnp.zeros(rates.shape, jnp.float32), inputs)
    return outputs

def reference(qkv_first, short_first, medium_filter, out_weight, residual_in, norm_gain, in_weight, short_second, rates, residues, skip_gain):
    padded_first = jnp.pad(qkv_first, ((0, 0), (2, 0), (0, 0)))
    features = featurize(padded_first, short_first)
    gated_first = (features[1] * features[2]).astype(jnp.bfloat16)
    mixed_first = (features[0] * medium_reference(gated_first, medium_filter)).astype(jnp.bfloat16)
    channels = D // N_TP
    summed = jnp.zeros(residual_in.shape, jnp.float32)
    for group_index in range(N_TP):
        lower = group_index * channels
        partial_value = jnp.dot(mixed_first[:, lower:lower + channels], out_weight[lower:lower + channels], preferred_element_type=jnp.float32)
        summed = summed + lax.optimization_barrier(partial_value.astype(jnp.bfloat16)).astype(jnp.float32)
    hidden = (residual_in.astype(jnp.float32) + summed).astype(jnp.bfloat16)
    hidden_values = hidden.astype(jnp.float32)
    mean_square = lax.optimization_barrier(jnp.sum(hidden_values * hidden_values, axis=1)) / D
    normed = (hidden_values * lax.rsqrt(mean_square + EPSILON)[:, None] * norm_gain.astype(jnp.float32)).astype(jnp.bfloat16)
    qkv_second = jnp.stack([jnp.dot(normed, in_weight[which], preferred_element_type=jnp.float32).astype(jnp.bfloat16) for which in range(3)])
    padded_second = jnp.pad(qkv_second, ((0, 0), (2, 0), (0, 0)))
    features_second = featurize(padded_second, short_second)
    gated_second = (features_second[1] * features_second[2]).astype(jnp.bfloat16)
    modal = modal_reference(gated_second, rates, residues)
    mixed = (features_second[0] * (modal + skip_gain * gated_second.astype(jnp.float32))).astype(jnp.bfloat16)
    return (hidden, mixed)
```

```python
import functools

import jax
import jax.numpy as jnp
from jax import lax
from jax.experimental import pallas as pl
from jax.experimental.pallas import tpu as pltpu
from jax.sharding import PartitionSpec as P

HALO = 144


def conv_kernel(prev_ref, cur_ref, taps_ref, filt_ref, out_ref, k_ref, v_ref, g_ref, e_ref, y_ref):
    length = cur_ref.shape[1]
    lag = filt_ref.shape[0]
    block = length // 8
    keep = lag + 8
    for ref, m in ((k_ref, 1), (v_ref, 2)):
        ref[:keep, :] = prev_ref[m, prev_ref.shape[1] - keep :, :].astype(jnp.float32)
        ref[keep:, :] = cur_ref[m].astype(jnp.float32)

    def feature(ref, m, at, rows):
        return (
            taps_ref[m, 0:1, :] * ref[pl.ds(at, rows), :]
            + taps_ref[m, 1:2, :] * ref[pl.ds(at - 1, rows), :]
            + taps_ref[m, 2:3, :] * ref[pl.ds(at - 2, rows), :]
        )

    for r in range(0, lag + length, 128):
        gated = feature(k_ref, 1, r + 8, 128) * feature(v_ref, 2, r + 8, 128)
        g_ref[r : r + 128, :] = gated.astype(jnp.bfloat16).astype(jnp.float32)
    for k in range(block + lag):
        e_ref[k] = g_ref[pl.ds(k, 8, stride=block), :]
    tile, step = 16, 8
    for i0 in range(0, block, tile):

        def taps(n, acc, i0=i0):
            j0 = n * step
            base = lag + i0 - (step - 1)
            held = [e_ref[base + s - j0] for s in range(tile + step - 1)]
            acc = list(acc)
            for s in range(step):
                weight = jnp.broadcast_to(filt_ref[pl.ds(j0 + s, 1), :], (8, 128))
                for i in range(tile):
                    acc[i] = acc[i] + weight * held[i + step - 1 - s]
            return tuple(acc)

        zero = jnp.zeros((8, 128), jnp.float32)
        acc = lax.fori_loop(0, lag // step, taps, (zero,) * tile)
        for i in range(tile):
            y_ref[pl.ds(i0 + i, 8, stride=block), :] = acc[i]
    k_ref[:keep, :] = prev_ref[0, prev_ref.shape[1] - keep :, :].astype(jnp.float32)
    k_ref[keep:, :] = cur_ref[0].astype(jnp.float32)
    for r in range(0, length, 128):
        query = feature(k_ref, 0, keep + r, 128)
        out_ref[r : r + 128, :] = (query * y_ref[r : r + 128, :]).astype(jnp.bfloat16)


def medium(prev, cur, taps, filt):
    length, channels = cur.shape[1:]
    lag = filt.shape[0]
    return pl.pallas_call(
        conv_kernel,
        out_shape=jax.ShapeDtypeStruct((length, channels), jnp.bfloat16),
        grid=(channels // 128,),
        in_specs=[
            pl.BlockSpec((3, prev.shape[1], 128), lambda g: (0, 0, g)),
            pl.BlockSpec((3, length, 128), lambda g: (0, 0, g)),
            pl.BlockSpec((3, 3, 128), lambda g: (0, 0, g)),
            pl.BlockSpec((lag, 128), lambda g: (0, g)),
        ],
        out_specs=pl.BlockSpec((length, 128), lambda g: (0, g)),
        scratch_shapes=[
            pltpu.VMEM((length + lag + 8, 128), jnp.float32),
            pltpu.VMEM((length + lag + 8, 128), jnp.float32),
            pltpu.VMEM((length + lag, 128), jnp.float32),
            pltpu.VMEM((length // 8 + lag, 8, 128), jnp.float32),
            pltpu.VMEM((length, 128), jnp.float32),
        ],
        name="medium",
    )(prev, cur, taps, filt)


def featurize_into(prev_ref, lower_ref, upper_ref, taps_ref, m, x_ref):
    half = lower_ref.shape[1]
    x_ref[:8, :] = prev_ref[m, prev_ref.shape[1] - 8 :, :].astype(jnp.float32)
    x_ref[8 : half + 8, :] = lower_ref[m].astype(jnp.float32)
    x_ref[half + 8 :, :] = upper_ref[m].astype(jnp.float32)

    def at(r, rows):
        return (
            taps_ref[m, 0:1, :] * x_ref[pl.ds(r + 8, rows), :]
            + taps_ref[m, 1:2, :] * x_ref[pl.ds(r + 7, rows), :]
            + taps_ref[m, 2:3, :] * x_ref[pl.ds(r + 6, rows), :]
        )

    return at


def scan_kernel(prev_ref, lower_ref, upper_ref, taps_ref, rates_ref, u_ref, starts_ref, end_ref, k_ref, v_ref, g_ref, p_ref):
    poles = rates_ref.shape[0]
    length = 2 * lower_ref.shape[1]
    block = length // 8
    kf = featurize_into(prev_ref, lower_ref, upper_ref, taps_ref, 1, k_ref)
    vf = featurize_into(prev_ref, lower_ref, upper_ref, taps_ref, 2, v_ref)
    for r in range(0, length, 128):
        gated = (kf(r, 128) * vf(r, 128)).astype(jnp.bfloat16)
        g_ref[r : r + 128, :] = gated.astype(jnp.float32)
    for i in range(block):
        u_ref[i] = g_ref[pl.ds(i, 8, stride=block), :]
    pole = [jnp.broadcast_to(jnp.exp(-rates_ref[n : n + 1, :]), (8, 128)) for n in range(poles)]

    def advance(i, states):
        states = list(states)
        for s in range(2):
            u = u_ref[i * 2 + s]
            states = [p * a + u for p, a in zip(pole, states)]
        return tuple(states)

    zero = jnp.zeros((8, 128), jnp.float32)
    states = lax.fori_loop(0, block // 2, advance, (zero,) * poles)
    for n in range(poles):
        decay = jnp.exp(-rates_ref[n : n + 1, :] * block)
        p_ref[...] = states[n]
        run = jnp.zeros((1, 128), jnp.float32)
        for b in range(8):
            starts_ref[n, b : b + 1, :] = run
            run = decay * run + p_ref[b : b + 1, :]
        end_ref[n : n + 1, :] = run.astype(jnp.bfloat16)


def modal_scan(prev, lower, upper, taps, rates):
    half, channels = lower.shape[1:]
    length = 2 * half
    poles = rates.shape[0]
    return pl.pallas_call(
        scan_kernel,
        out_shape=(
            jax.ShapeDtypeStruct((length // 8, 8, channels), jnp.float32),
            jax.ShapeDtypeStruct((poles, 8, channels), jnp.float32),
            jax.ShapeDtypeStruct((poles, channels), jnp.bfloat16),
        ),
        grid=(channels // 128,),
        in_specs=[
            pl.BlockSpec((3, prev.shape[1], 128), lambda g: (0, 0, g)),
            pl.BlockSpec((3, half, 128), lambda g: (0, 0, g)),
            pl.BlockSpec((3, half, 128), lambda g: (0, 0, g)),
            pl.BlockSpec((3, 3, 128), lambda g: (0, 0, g)),
            pl.BlockSpec((poles, 128), lambda g: (0, g)),
        ],
        out_specs=(
            pl.BlockSpec((length // 8, 8, 128), lambda g: (0, 0, g)),
            pl.BlockSpec((poles, 8, 128), lambda g: (0, 0, g)),
            pl.BlockSpec((poles, 128), lambda g: (0, g)),
        ),
        scratch_shapes=[
            pltpu.VMEM((length + 8, 128), jnp.float32),
            pltpu.VMEM((length + 8, 128), jnp.float32),
            pltpu.VMEM((length, 128), jnp.float32),
            pltpu.VMEM((8, 128), jnp.float32),
        ],
        name="modal_scan",
    )(prev, lower, upper, taps, rates)


def finish_kernel(prev_ref, lower_ref, upper_ref, taps_ref, rates_ref, residues_ref, skip_ref, u_ref, starts_ref, enter_ref, out_ref, q_ref, y_ref):
    poles = rates_ref.shape[0]
    length = 2 * lower_ref.shape[1]
    block = length // 8
    pole = [jnp.broadcast_to(jnp.exp(-rates_ref[n : n + 1, :]), (8, 128)) for n in range(poles)]
    weight = [jnp.broadcast_to(residues_ref[n : n + 1, :], (8, 128)) for n in range(poles)]
    skip = jnp.broadcast_to(skip_ref[...], (8, 128))
    place = lax.broadcasted_iota(jnp.int32, (8, 128), 0).astype(jnp.float32) * block
    states = tuple(
        starts_ref[n] + jnp.exp(-rates_ref[n : n + 1, :] * place) * enter_ref[n : n + 1, :]
        for n in range(poles)
    )

    def advance(i, states):
        u = u_ref[i]
        states = [p * a + u for p, a in zip(pole, states)]
        parts = [w * a for w, a in zip(weight, states)] + [skip * u]
        while len(parts) > 1:
            parts = [a + b for a, b in zip(parts[::2], parts[1::2])] + parts[len(parts) & ~1 :]
        y_ref[pl.ds(i, 8, stride=block), :] = parts[0]
        return tuple(states)

    lax.fori_loop(0, block, advance, states)
    qf = featurize_into(prev_ref, lower_ref, upper_ref, taps_ref, 0, q_ref)
    for r in range(0, length, 128):
        out_ref[r : r + 128, :] = (qf(r, 128) * y_ref[r : r + 128, :]).astype(jnp.bfloat16)


def modal_finish(prev, lower, upper, taps, rates, residues, skip, u, starts, enter):
    half, channels = lower.shape[1:]
    length = 2 * half
    poles = rates.shape[0]
    return pl.pallas_call(
        finish_kernel,
        out_shape=jax.ShapeDtypeStruct((length, channels), jnp.bfloat16),
        grid=(channels // 128,),
        in_specs=[
            pl.BlockSpec((1, prev.shape[1], 128), lambda g: (0, 0, g)),
            pl.BlockSpec((1, half, 128), lambda g: (0, 0, g)),
            pl.BlockSpec((1, half, 128), lambda g: (0, 0, g)),
            pl.BlockSpec((3, 3, 128), lambda g: (0, 0, g)),
            pl.BlockSpec((poles, 128), lambda g: (0, g)),
            pl.BlockSpec((poles, 128), lambda g: (0, g)),
            pl.BlockSpec((1, 128), lambda g: (0, g)),
            pl.BlockSpec((length // 8, 8, 128), lambda g: (0, 0, g)),
            pl.BlockSpec((poles, 8, 128), lambda g: (0, 0, g)),
            pl.BlockSpec((poles, 128), lambda g: (0, g)),
        ],
        out_specs=pl.BlockSpec((length, 128), lambda g: (0, g)),
        scratch_shapes=[
            pltpu.VMEM((length + 8, 128), jnp.float32),
            pltpu.VMEM((length, 128), jnp.float32),
        ],
        name="modal_finish",
    )(prev, lower, upper, taps, rates, residues, skip.reshape(1, channels), u, starts, enter)


D = 4096
EPSILON = 1e-05
ROWS = 512


def x_pairs(d):
    return [(c, c // 4 * 4 + (c + d) % 4) for c in range(16)]


def y_pairs(d):
    return [(c, (c + 4 * d) % 16) for c in range(16)]


def z_pairs(d):
    return [(t, (t + 2 * d) % 8) for t in range(8)]


def core_pairs():
    return [(t, t ^ 1) for t in range(8)]


def ring_gather(a, axis, pairs, cut):
    after = lax.ppermute(a, axis, pairs(-1))
    before = lax.ppermute(a, axis, pairs(1))
    half = a.shape[cut] // 2
    low = lax.ppermute(lax.slice_in_dim(after, 0, half, axis=cut), axis, pairs(-1))
    high = lax.ppermute(lax.slice_in_dim(before, half, 2 * half, axis=cut), axis, pairs(1))
    return a, after, low, high, before


def plane_gather(a, first, second):
    own, after, low, high, before = ring_gather(a, "ctx", first, 1)
    opposite = jnp.concatenate([low, high], axis=1)
    line = jnp.stack([own, after, opposite, before])
    return ring_gather(line, "ctx", second, 0)


def token_gather(a):
    pieces = ring_gather(a, "tp", z_pairs, 0)
    swapped = [lax.ppermute(p, "tp", core_pairs()) for p in pieces]
    return (*pieces, *swapped)


def matmul_kernel(norm, place_ref, *refs):
    acts, refs = refs[:10], refs[10:]
    west, refs = refs[:5], refs[5:]
    south, refs = refs[:5], refs[5:]
    if norm:
        out_ref, act_ref, scale_ref = refs
    else:
        extra_ref, out_ref, act_ref = refs
    y, x, z, core = (place_ref[n] for n in range(4))
    rows = act_ref.shape[1]

    @pl.when(pl.program_id(0) == 0)
    def _():
        if norm:
            scale_ref[...] = jnp.zeros_like(scale_ref)
        for s in range(2):
            for dz in range(4):
                held = [acts[5 * s + n] for n in ((0,), (1,), (2, 3), (4,))[dz]]
                part = rows // len(held)
                for n, ref in enumerate(held):
                    for h in range(2):
                        block = ref[:, h * 256 : h * 256 + 256]
                        at = (z + dz) % 4 * 4 + (core ^ s) * 2 + h
                        act_ref[at, n * part : n * part + part, :] = block
                        if norm:
                            wide = block.astype(jnp.float32)
                            wide = wide * wide
                            scale_ref[n * part : n * part + part, :] += wide[:, :128] + wide[:, 128:]
        if norm:
            total = jnp.sum(scale_ref[...], axis=1, keepdims=True)
            scale_ref[...] = jnp.broadcast_to(lax.rsqrt(total / D + EPSILON), scale_ref.shape)

    for side, weights in enumerate((west, south)):
        total = jnp.zeros((rows, 256), jnp.float32)
        for outer in range(4):
            left, right = [], []
            for inner in range(4):
                dy, dx = (outer, inner) if side == 0 else (inner, outer)
                left.append(act_ref[(y + dy) % 4 * 4 + (x + dx) % 4])
                if outer == 2:
                    right.append(weights[2 + inner // 2][inner % 2, 0])
                else:
                    right.append(weights[(0, 1, 2, 4)[outer]][inner, 0])
            total = total + jnp.dot(
                jnp.concatenate(left, axis=1),
                jnp.concatenate(right, axis=0),
                preferred_element_type=jnp.float32,
            )
        lanes = slice(side * 256, side * 256 + 256)
        if norm:
            scale = scale_ref[...]
            scale = jnp.concatenate([scale, scale], axis=1)
            out_ref[0, :, lanes] = (total * scale).astype(jnp.bfloat16)
        else:
            wide = extra_ref[:, lanes].astype(jnp.float32)
            out_ref[0, :, lanes] = (wide + total).astype(jnp.bfloat16)


def matmul(place, acts, west, south, residual=None, at=0):
    norm = residual is None
    units = west[0].shape[1]
    rows, channels = acts[0].shape
    once = pl.Buffered(1)
    specs = [pl.BlockSpec(a.shape, lambda j, _: (0, 0), pipeline_mode=once) for a in acts]
    for w in (*west, *south):
        specs.append(pl.BlockSpec((w.shape[0], 1, 256, 256), lambda j, _: (0, j, 0, 0)))
    operands = [*acts, *west, *south]
    scratch = [pltpu.VMEM((16, rows, 256), jnp.bfloat16)]
    if norm:
        scratch.append(pltpu.VMEM((rows, 128), jnp.float32))
    else:
        specs.append(pl.BlockSpec((rows, channels), lambda j, _: (at, 0), pipeline_mode=once))
        operands.append(residual)
    return pl.pallas_call(
        functools.partial(matmul_kernel, norm),
        out_shape=jax.ShapeDtypeStruct((units, rows, channels), jnp.bfloat16),
        grid_spec=pltpu.PrefetchScalarGridSpec(
            num_scalar_prefetch=1,
            grid=(units,),
            in_specs=specs,
            out_specs=pl.BlockSpec((1, rows, channels), lambda j, _: (j, 0, 0)),
            scratch_shapes=scratch,
        ),
        name="project" if norm else "mix",
    )(place, *operands)


def on_device(
    qkv_first,
    short_first,
    medium_filter,
    out_weight,
    residual_in,
    norm_gain,
    in_weight,
    short_second,
    rates,
    residues,
    skip_gain,
):
    length = qkv_first.shape[1]
    c = lax.axis_index("ctx")
    t = lax.axis_index("tp")
    x, y, core, z = c % 4, c // 4, t % 2, t // 2
    place = jnp.stack([y, x, z, core]).astype(jnp.int32)
    ahead = [(i, i + 1) for i in range(15)]

    rim = lax.ppermute(qkv_first[:, length - HALO :], "ctx", ahead)

    gains = jnp.broadcast_to(norm_gain.reshape(2, 1, 256), (2, 16, 256))
    packed = jnp.concatenate([out_weight.reshape(2, 256, 256), gains], axis=1)
    odd = c % 2
    turned = []
    for k in range(2):
        pairs = []
        for cc in range(16):
            for tt in range(8):
                to = (2 * tt + (cc + k) % 2, cc // 2)
                pairs.append((cc * 8 + tt, to[0] * 8 + to[1]))
        mine = lax.dynamic_index_in_dim(packed, (odd + k) % 2, 0, False)
        turned.append(lax.ppermute(mine, ("ctx", "tp"), pairs))
    first = jnp.where(odd == 0, turned[0], turned[1])
    second = jnp.where(odd == 0, turned[1], turned[0])
    own_gain = turned[0][256].astype(jnp.float32)
    out_west = plane_gather(first[None, :256], x_pairs, y_pairs)
    out_south = plane_gather(second[None, :256], y_pairs, x_pairs)
    scaled = (in_weight.astype(jnp.float32) * own_gain[None, :, None]).astype(jnp.bfloat16)
    in_west = plane_gather(scaled[:, :, :256], x_pairs, y_pairs)
    in_south = plane_gather(scaled[:, :, 256:], y_pairs, x_pairs)

    filt = medium_filter.T.astype(jnp.float32)
    upper = medium(qkv_first[:, ROWS - HALO : ROWS], qkv_first[:, ROWS:], short_first, filt)
    upper_pieces = token_gather(upper)
    lower = medium(rim, qkv_first[:, :ROWS], short_first, filt)
    lower_pieces = token_gather(lower)
    hidden_upper = matmul(place, upper_pieces, out_west, out_south, residual_in, 1)[0]
    hidden_upper_pieces = token_gather(hidden_upper)
    hidden_lower = matmul(place, lower_pieces, out_west, out_south, residual_in, 0)[0]
    hidden_lower_pieces = token_gather(hidden_lower)
    qkv_upper = matmul(place, hidden_upper_pieces, in_west, in_south)
    edge = lax.ppermute(qkv_upper[:, ROWS - 16 :], "ctx", ahead)
    qkv_lower = matmul(place, hidden_lower_pieces, in_west, in_south)
    hidden = jnp.concatenate([hidden_lower, hidden_upper], axis=0)

    u, starts, end = modal_scan(edge, qkv_lower, qkv_upper, short_second, rates)
    log_decay = -rates * length

    def decay(k):
        return jnp.exp(log_decay * k.astype(jnp.float32))

    along = [end] + [lax.ppermute(end, "ctx", x_pairs(-d)) for d in (1, 2, 3)]
    row = jnp.zeros_like(rates)
    enter = jnp.zeros_like(rates)
    for d, e in enumerate(along):
        at = (x + d) % 4
        wide = e.astype(jnp.float32)
        row = row + decay(3 - at) * wide
        enter = enter + jnp.where(at < x, decay(jnp.maximum(x - 1 - at, 0)), 0.0) * wide
    row = row.astype(jnp.bfloat16)
    for d in (1, 2, 3):
        e = lax.ppermute(row, "ctx", y_pairs(-d))
        at = (y + d) % 4
        enter = enter + jnp.where(
            at < y, decay(x + 4 * jnp.maximum(y - 1 - at, 0)), 0.0
        ) * e.astype(jnp.float32)
    mixed = modal_finish(
        edge, qkv_lower, qkv_upper, short_second, rates, residues, skip_gain, u, starts, enter
    )
    return (hidden, mixed)


def solution(mesh):
    placed = (
        P(None, "ctx", "tp"),
        P(None, None, "tp"),
        P("tp", None),
        P("tp", "ctx"),
        P("ctx", "tp"),
        P("tp"),
        P(None, "ctx", "tp"),
        P(None, None, "tp"),
        P(None, "tp"),
        P(None, "tp"),
        P("tp"),
    )
    return jax.shard_map(
        on_device,
        mesh=mesh,
        in_specs=placed,
        out_specs=(P("ctx", "tp"), P("ctx", "tp")),
        check_vma=False,
    )
```

```python
import functools


import jax
import jax.numpy as jnp
from jax import lax
from jax.experimental import pallas as pl
from jax.experimental.pallas import tpu as pltpu
from jax.sharding import PartitionSpec as P

HALO = 144


def conv_kernel(extra, prev_ref, cur_ref, taps_ref, filt_ref, gain_ref, out_ref, k_ref, v_ref, g_ref, d_ref, r_ref, y_ref):
    length = cur_ref.shape[1]
    lag = 4 * filt_ref.shape[1]
    block = length // 8
    keep = lag + 8
    for ref, m in ((k_ref, 1), (v_ref, 2)):
        ref[:keep, :] = prev_ref[m, prev_ref.shape[1] - keep :, :].astype(jnp.float32)
        ref[keep:, :] = cur_ref[m].astype(jnp.float32)

    def feature(ref, m, at, rows):
        return (
            taps_ref[m, 0:1, :] * ref[pl.ds(at, rows), :]
            + taps_ref[m, 1:2, :] * ref[pl.ds(at - 1, rows), :]
            + taps_ref[m, 2:3, :] * ref[pl.ds(at - 2, rows), :]
        )

    for r in range(0, lag + length, 128):
        gated = feature(k_ref, 1, r + 8, 128) * feature(v_ref, 2, r + 8, 128)
        g_ref[r : r + 128, :] = gated.astype(jnp.bfloat16).astype(jnp.float32)

    def spread(k):
        return g_ref[pl.ds(k, 8, stride=block), :]

    for n in range((block + lag) // 4):
        e = [spread(4 * n + q) for q in range(4)]
        for w, (first, second) in enumerate(((e[0], e[2]), (e[1], e[3]), (e[0] + e[1], e[2] + e[3]))):
            d_ref[3 * w, n] = first
            d_ref[3 * w + 1, n] = second
            d_ref[3 * w + 2, n] = first + second
    count = block // 4 + 1
    base = lag // 4 - 1

    def short(n, carry):
        acc = [None] * count
        for q in range(lag // 4):
            weight = jnp.broadcast_to(filt_ref[n, pl.ds(q, 1), :], (8, 128))
            for i in range(count):
                term = weight * d_ref[n, base + i - q]
                acc[i] = term if q == 0 else acc[i] + term
        for i in range(count):
            r_ref[n, i] = acc[i]
        return carry

    lax.fori_loop(0, 9, short, 0)

    def joined(w, i):
        if i % 2:
            return r_ref[3 * w, i // 2 + 1] + r_ref[3 * w + 1, i // 2]
        return r_ref[3 * w + 2, i // 2] - r_ref[3 * w, i // 2] - r_ref[3 * w + 1, i // 2]

    late = joined(1, 0)
    for i in range(block // 2):
        even, odd, both = (joined(w, i + 1) for w in range(3))
        y_ref[pl.ds(2 * i, 8, stride=block), :] = even + late
        y_ref[pl.ds(2 * i + 1, 8, stride=block), :] = both - even - odd
        late = odd
    k_ref[:keep, :] = prev_ref[0, prev_ref.shape[1] - keep :, :].astype(jnp.float32)
    k_ref[keep:, :] = cur_ref[0].astype(jnp.float32)
    for r in range(0, length, 128):
        query = feature(k_ref, 0, keep + r, 128)
        out_ref[r : r + 128, :] = (query * y_ref[r : r + 128, :]).astype(jnp.bfloat16)
    if extra:
        out_ref[length:, :] = jnp.broadcast_to(gain_ref[...], (extra, 128))


def medium(prev, prev_rows, prev_at, qkv, at, taps, filt, gain, extra):
    length, channels = ROWS, qkv.shape[2]
    lag = 4 * filt.shape[1]
    return pl.pallas_call(
        functools.partial(conv_kernel, extra),
        out_shape=jax.ShapeDtypeStruct((length + extra, channels), jnp.bfloat16),
        grid=(channels // 128,),
        in_specs=[
            pl.BlockSpec((3, prev_rows, 128), lambda g: (0, prev_at, g)),
            pl.BlockSpec((3, length, 128), lambda g: (0, at, g)),
            pl.BlockSpec((3, 3, 128), lambda g: (0, 0, g)),
            pl.BlockSpec((9, lag // 4, 128), lambda g: (0, 0, g)),
            pl.BlockSpec((1, 128), lambda g: (0, g)),
        ],
        out_specs=pl.BlockSpec((length + extra, 128), lambda g: (0, g)),
        scratch_shapes=[
            pltpu.VMEM((length + lag + 8, 128), jnp.float32),
            pltpu.VMEM((length + lag + 8, 128), jnp.float32),
            pltpu.VMEM((length + lag, 128), jnp.float32),
            pltpu.VMEM((9, (length // 8 + lag) // 4, 8, 128), jnp.float32),
            pltpu.VMEM((9, length // 32 + 1, 8, 128), jnp.float32),
            pltpu.VMEM((length, 128), jnp.float32),
        ],
        compiler_params=pltpu.CompilerParams(vmem_limit_bytes=16 << 20),
        name="medium",
    )(prev, qkv, taps, filt, gain.reshape(1, channels))


def split_taps(filters):
    f = filters.T.astype(jnp.float32).reshape(-1, 4, filters.shape[0])
    rows = []
    for first, second in ((f[:, 0], f[:, 2]), (f[:, 1], f[:, 3]), (f[:, 0] + f[:, 1], f[:, 2] + f[:, 3])):
        rows += [first, second, first + second]
    return jnp.stack(rows)


def featurize_into(edge_ref, lower_ref, upper_ref, at_upper, at_lower, taps_ref, m, x_ref):
    half = lower_ref.shape[1]
    x_ref[:8, :] = edge_ref[at_upper, edge_ref.shape[1] - 8 :, :].astype(jnp.float32)
    x_ref[8 : half + 8, :] = lower_ref[at_lower].astype(jnp.float32)
    x_ref[half + 8 :, :] = upper_ref[at_upper].astype(jnp.float32)

    def at(r, rows):
        return (
            taps_ref[m, 0:1, :] * x_ref[pl.ds(r + 8, rows), :]
            + taps_ref[m, 1:2, :] * x_ref[pl.ds(r + 7, rows), :]
            + taps_ref[m, 2:3, :] * x_ref[pl.ds(r + 6, rows), :]
        )

    return at


def scan_kernel(
    edge_ref, lower_ref, upper_ref, taps_ref, rates_ref, u_ref, starts_ref, end_ref, k_ref, v_ref, g_ref, p_ref
):
    poles = rates_ref.shape[0]
    length = 2 * lower_ref.shape[1]
    block = length // 8
    kf = featurize_into(edge_ref, lower_ref, upper_ref, 1, 0, taps_ref, 1, k_ref)
    vf = featurize_into(edge_ref, lower_ref, upper_ref, 2, 1, taps_ref, 2, v_ref)
    for r in range(0, length, 128):
        gated = (kf(r, 128) * vf(r, 128)).astype(jnp.bfloat16)
        g_ref[r : r + 128, :] = gated.astype(jnp.float32)
    for i in range(block):
        u_ref[i] = g_ref[pl.ds(i, 8, stride=block), :]
    pole = [jnp.broadcast_to(jnp.exp(-rates_ref[n : n + 1, :]), (8, 128)) for n in range(poles)]

    def advance(i, states):
        states = list(states)
        for s in range(4):
            u = u_ref[i * 4 + s]
            states = [p * a + u for p, a in zip(pole, states)]
        return tuple(states)

    zero = jnp.zeros((8, 128), jnp.float32)
    states = lax.fori_loop(0, block // 4, advance, (zero,) * poles)
    for n in range(poles):
        decay = jnp.exp(-rates_ref[n : n + 1, :] * block)
        p_ref[...] = states[n]
        run = jnp.zeros((1, 128), jnp.float32)
        for b in range(8):
            starts_ref[n, b : b + 1, :] = run
            run = decay * run + p_ref[b : b + 1, :]
        end_ref[n : n + 1, :] = run.astype(jnp.bfloat16)


def modal_scan(edge, lower, upper, taps, rates):
    half, channels = lower.shape[1:]
    length = 2 * half
    poles = rates.shape[0]
    line = lambda rows: pl.BlockSpec((rows, 128), lambda g: (0, g))
    cube = lambda rows: pl.BlockSpec((rows, 8, 128), lambda g: (0, 0, g))
    return pl.pallas_call(
        scan_kernel,
        out_shape=(
            jax.ShapeDtypeStruct((length // 8, 8, channels), jnp.float32),
            jax.ShapeDtypeStruct((poles, 8, channels), jnp.float32),
            jax.ShapeDtypeStruct((poles, channels), jnp.bfloat16),
        ),
        grid=(channels // 128,),
        in_specs=[
            pl.BlockSpec((3, 16, 128), lambda g: (0, 0, g)),
            pl.BlockSpec((2, half, 128), lambda g: (0, 0, g)),
            pl.BlockSpec((3, half, 128), lambda g: (0, 0, g)),
            pl.BlockSpec((3, 3, 128), lambda g: (0, 0, g)),
            line(poles),
        ],
        out_specs=(cube(length // 8), cube(poles), line(poles)),
        scratch_shapes=[
            pltpu.VMEM((length + 8, 128), jnp.float32),
            pltpu.VMEM((length + 8, 128), jnp.float32),
            pltpu.VMEM((length, 128), jnp.float32),
            pltpu.VMEM((8, 128), jnp.float32),
        ],
        compiler_params=pltpu.CompilerParams(vmem_limit_bytes=16 << 20),
        name="modal_scan",
    )(edge, lower, upper, taps, rates)


def finish_kernel(
    edge_ref, lower_ref, upper_ref, taps_ref, rates_ref, residues_ref, skip_ref, u_ref, starts_ref, enter_ref, out_ref, q_ref, y_ref
):
    poles = rates_ref.shape[0]
    length = 2 * lower_ref.shape[1]
    block = length // 8
    pole = [jnp.broadcast_to(jnp.exp(-rates_ref[n : n + 1, :]), (8, 128)) for n in range(poles)]
    weight = [jnp.broadcast_to(residues_ref[n : n + 1, :], (8, 128)) for n in range(poles)]
    skip = jnp.broadcast_to(skip_ref[...], (8, 128))
    place = lax.broadcasted_iota(jnp.int32, (8, 128), 0).astype(jnp.float32) * block
    states = tuple(
        starts_ref[n] + jnp.exp(-rates_ref[n : n + 1, :] * place) * enter_ref[n : n + 1, :]
        for n in range(poles)
    )

    def advance(j, states):
        for s in range(4):
            i = j * 4 + s
            u = u_ref[i]
            states = [p * a + u for p, a in zip(pole, states)]
            parts = [w * a for w, a in zip(weight, states)] + [skip * u]
            while len(parts) > 1:
                parts = [a + b for a, b in zip(parts[::2], parts[1::2])] + parts[len(parts) & ~1 :]
            y_ref[pl.ds(i, 8, stride=block), :] = parts[0]
        return tuple(states)

    lax.fori_loop(0, block // 4, advance, states)
    qf = featurize_into(edge_ref, lower_ref, upper_ref, 0, 0, taps_ref, 0, q_ref)
    for r in range(0, length, 128):
        out_ref[r : r + 128, :] = (qf(r, 128) * y_ref[r : r + 128, :]).astype(jnp.bfloat16)


def modal_finish(edge, lower, upper, taps, rates, residues, skip, u, starts, enter):
    half, channels = lower.shape[1:]
    length = 2 * half
    poles = rates.shape[0]
    line = lambda rows: pl.BlockSpec((rows, 128), lambda g: (0, g))
    cube = lambda rows: pl.BlockSpec((rows, 8, 128), lambda g: (0, 0, g))
    return pl.pallas_call(
        finish_kernel,
        out_shape=jax.ShapeDtypeStruct((length, channels), jnp.bfloat16),
        grid=(channels // 128,),
        in_specs=[
            pl.BlockSpec((1, 16, 128), lambda g: (0, 0, g)),
            pl.BlockSpec((1, half, 128), lambda g: (0, 0, g)),
            pl.BlockSpec((1, half, 128), lambda g: (0, 0, g)),
            pl.BlockSpec((3, 3, 128), lambda g: (0, 0, g)),
            line(poles),
            line(poles),
            line(1),
            cube(length // 8),
            cube(poles),
            line(poles),
        ],
        out_specs=line(length),
        scratch_shapes=[
            pltpu.VMEM((length + 8, 128), jnp.float32),
            pltpu.VMEM((length, 128), jnp.float32),
        ],
        compiler_params=pltpu.CompilerParams(vmem_limit_bytes=16 << 20),
        name="modal_finish",
    )(edge, lower, upper, taps, rates, residues, skip.reshape(1, channels), u, starts, enter)


D = 4096
EPSILON = 1e-05
ROWS = 512
EXTRA = 16


def x_pairs(d):
    return [(c, c // 4 * 4 + (c + d) % 4) for c in range(16)]


def y_pairs(d):
    return [(c, (c + 4 * d) % 16) for c in range(16)]


def z_pairs(d):
    return [(t, (t + 2 * d) % 8) for t in range(8)]


def core_pairs():
    return [(t, t ^ 1) for t in range(8)]


def ring(a, axis, pairs):
    return [a] + [lax.ppermute(a, axis, pairs(-d)) for d in (1, 2, 3)]


def plane_gather(a, first, second):
    pieces = ring(a, "ctx", first)
    return ring(jnp.stack(pieces), "ctx", second)


def token_gather(a):
    pieces = ring(a, "tp", z_pairs)
    return (*pieces, *[lax.ppermute(p, "tp", core_pairs()) for p in pieces])


def mix_kernel(place_ref, *refs):
    acts, west, south, refs = refs[:8], refs[8:12], refs[12:16], refs[16:]
    residual_ref, out_ref, act_ref = refs
    y, x, z, core = (place_ref[n] for n in range(4))
    rows = act_ref.shape[1]
    for s in range(2):
        for dz in range(4):
            at = (z + dz) % 4 * 4 + (core ^ s) * 2
            for h in range(2):
                act_ref[at + h] = acts[4 * s + dz][:rows, h * 256 : h * 256 + 256]
    for side, weights in enumerate((west, south)):
        total = jnp.zeros((rows, 256), jnp.float32)
        for outer in range(4):
            left, right = [], []
            for inner in range(4):
                dy, dx = (outer, inner) if side == 0 else (inner, outer)
                left.append(act_ref[(y + dy) % 4 * 4 + (x + dx) % 4])
                right.append(weights[outer][inner])
            total = total + jnp.dot(
                jnp.concatenate(left, axis=1),
                jnp.concatenate(right, axis=0),
                preferred_element_type=jnp.float32,
            )
        lanes = slice(side * 256, side * 256 + 256)
        wide = residual_ref[:, lanes].astype(jnp.float32)
        out_ref[:, lanes] = (wide + total).astype(jnp.bfloat16)


def mix(place, acts, west, south, residual, at):
    rows, channels = ROWS, acts[0].shape[1]
    whole = lambda a: pl.BlockSpec(a.shape, lambda j, _: (0,) * a.ndim)
    return pl.pallas_call(
        mix_kernel,
        out_shape=jax.ShapeDtypeStruct((rows, channels), jnp.bfloat16),
        grid_spec=pltpu.PrefetchScalarGridSpec(
            num_scalar_prefetch=1,
            grid=(1,),
            in_specs=[whole(a) for a in (*acts, *west, *south)]
            + [pl.BlockSpec((rows, channels), lambda j, _: (at, 0))],
            out_specs=pl.BlockSpec((rows, channels), lambda j, _: (0, 0)),
            scratch_shapes=[pltpu.VMEM((16, rows, 256), jnp.bfloat16)],
        ),
        compiler_params=pltpu.CompilerParams(vmem_limit_bytes=40 << 20),
        name="mix",
    )(place, *acts, *west, *south, residual)


def collect_kernel(place_ref, *refs):
    acts, gains, (act_ref, scale_ref) = refs[:8], refs[8:16], refs[16:]
    z, core = place_ref[2], place_ref[3]
    squares = jnp.zeros(scale_ref.shape, jnp.float32)
    for s in range(2):
        for dz in range(4):
            wide = acts[4 * s + dz][...].astype(jnp.float32)
            gain = gains[4 * s + dz][:1, :].astype(jnp.float32)
            act_ref[(z + dz) % 4 * 2 + (core ^ s)] = (wide * gain).astype(jnp.bfloat16)
            wide = wide * wide
            for n in range(0, wide.shape[1], 128):
                squares = squares + wide[:, n : n + 128]
    total = jnp.sum(squares, axis=1, keepdims=True)
    scale_ref[...] = jnp.broadcast_to(lax.rsqrt(total / D + EPSILON), squares.shape)


def collect(place, acts, gains):
    rows, channels = acts[0].shape
    return pl.pallas_call(
        collect_kernel,
        out_shape=(
            jax.ShapeDtypeStruct((8, rows, channels), jnp.bfloat16),
            jax.ShapeDtypeStruct((rows, 128), jnp.float32),
        ),
        grid_spec=pltpu.PrefetchScalarGridSpec(
            num_scalar_prefetch=1,
            grid=(1,),
            in_specs=[pl.BlockSpec((rows, channels), lambda j, _: (0, 0)) for a in acts]
            + [pl.BlockSpec((EXTRA, channels), lambda j, _: (ROWS // EXTRA, 0)) for a in gains],
            out_specs=(
                pl.BlockSpec((8, rows, channels), lambda j, _: (0, 0, 0)),
                pl.BlockSpec((rows, 128), lambda j, _: (0, 0)),
            ),
        ),
        name="collect",
    )(place, *acts, *gains)


def project_kernel(act_ref, scale_ref, weight_ref, out_ref):
    left = jnp.concatenate([act_ref[n] for n in range(8)], axis=1)
    right = jnp.concatenate([weight_ref[n, 0] for n in range(16)], axis=0)
    total = jnp.dot(left, right, preferred_element_type=jnp.float32)
    scale = jnp.concatenate([scale_ref[...], scale_ref[...]], axis=1)
    out_ref[0] = (total * scale).astype(jnp.bfloat16)


def project(act, scale, weight, start, count):
    blocks, rows, channels = act.shape
    return pl.pallas_call(
        project_kernel,
        out_shape=jax.ShapeDtypeStruct((count, rows, channels), jnp.bfloat16),
        grid=(count, channels // 256),
        in_specs=[
            pl.BlockSpec((blocks, rows, channels), lambda m, n: (0, 0, 0)),
            pl.BlockSpec((rows, 128), lambda m, n: (0, 0)),
            pl.BlockSpec((16, 1, 256, 256), lambda m, n: (0, m + start, 0, n)),
        ],
        out_specs=pl.BlockSpec((1, rows, 256), lambda m, n: (m, 0, n)),
        name="project",
    )(act, scale, weight)


def on_device(
    qkv_first,
    short_first,
    medium_filter,
    out_weight,
    residual_in,
    norm_gain,
    in_weight,
    short_second,
    rates,
    residues,
    skip_gain,
):
    length = qkv_first.shape[1]
    c = lax.axis_index("ctx")
    t = lax.axis_index("tp")
    x, y, core, z = c % 4, c // 4, t % 2, t // 2
    place = jnp.stack([y, x, z, core]).astype(jnp.int32)
    ahead = [(i, i + 1) for i in range(15)]

    rim = lax.ppermute(qkv_first[:, length - HALO :], "ctx", ahead)

    packed = out_weight.reshape(2, 256, 256)
    odd = c % 2
    turned = []
    for k in range(2):
        pairs = []
        for cc in range(16):
            for tt in range(8):
                to = (2 * tt + (cc + k) % 2, cc // 2)
                pairs.append((cc * 8 + tt, to[0] * 8 + to[1]))
        mine = lax.dynamic_index_in_dim(packed, (odd + k) % 2, 0, False)
        turned.append(lax.ppermute(mine, ("ctx", "tp"), pairs))
    first = jnp.where(odd == 0, turned[0], turned[1])
    second = jnp.where(odd == 0, turned[1], turned[0])
    weight = lax.all_gather(in_weight, "ctx")
    out_west = plane_gather(first, x_pairs, y_pairs)
    out_south = plane_gather(second, y_pairs, x_pairs)

    filt = split_taps(medium_filter)
    upper = medium(qkv_first, 256, 1, qkv_first, 1, short_first, filt, norm_gain, EXTRA)
    upper_pieces = token_gather(upper)
    lower = medium(rim, HALO, 0, qkv_first, 0, short_first, filt, norm_gain, 0)
    lower_pieces = token_gather(lower)
    hidden_upper = mix(place, upper_pieces, out_west, out_south, residual_in, 1)
    hidden_upper_pieces = token_gather(hidden_upper)
    hidden_lower = mix(place, lower_pieces, out_west, out_south, residual_in, 0)
    hidden_lower_pieces = token_gather(hidden_lower)
    hidden = jnp.concatenate([hidden_lower, hidden_upper], axis=0)
    act, scale = collect(place, hidden_upper_pieces, upper_pieces)
    qkv_upper = project(act, scale, weight, 0, 3)
    edge = lax.ppermute(qkv_upper[:, ROWS - 16 :], "ctx", ahead)
    act, scale = collect(place, hidden_lower_pieces, upper_pieces)
    kv_lower = project(act, scale, weight, 1, 2)
    u, starts, end = modal_scan(edge, kv_lower, qkv_upper, short_second, rates)
    log_decay = -rates * length

    def decay(k):
        return jnp.exp(log_decay * k.astype(jnp.float32))

    along = [end] + [lax.ppermute(end, "ctx", x_pairs(-d)) for d in (1, 2, 3)]
    row = jnp.zeros_like(rates)
    enter = jnp.zeros_like(rates)
    for d, e in enumerate(along):
        at = (x + d) % 4
        wide = e.astype(jnp.float32)
        row = row + decay(3 - at) * wide
        enter = enter + jnp.where(at < x, decay(jnp.maximum(x - 1 - at, 0)), 0.0) * wide
    row = row.astype(jnp.bfloat16)
    for d in (1, 2, 3):
        e = lax.ppermute(row, "ctx", y_pairs(-d))
        at = (y + d) % 4
        enter = enter + jnp.where(
            at < y, decay(x + 4 * jnp.maximum(y - 1 - at, 0)), 0.0
        ) * e.astype(jnp.float32)
    q_lower = project(act, scale, weight, 0, 1)
    mixed = modal_finish(
        edge, q_lower, qkv_upper, short_second, rates, residues, skip_gain, u, starts, enter
    )
    return (hidden, mixed)


def solution(mesh):
    placed = (
        P(None, "ctx", "tp"),
        P(None, None, "tp"),
        P("tp", None),
        P("tp", "ctx"),
        P("ctx", "tp"),
        P("tp"),
        P(None, "ctx", "tp"),
        P(None, None, "tp"),
        P(None, "tp"),
        P(None, "tp"),
        P("tp"),
    )
    return jax.shard_map(
        on_device,
        mesh=mesh,
        in_specs=placed,
        out_specs=(P("ctx", "tp"), P("ctx", "tp")),
        check_vma=False,
    )
```

```python
import jax
import jax.numpy as jnp
from jax import lax
from jax.experimental import pallas as pl
from jax.experimental.pallas import tpu as pltpu
from jax.sharding import PartitionSpec as P

HALO = 144


def conv_kernel(prev_ref, cur_ref, taps_ref, filt_ref, *refs):
    out_ref, k_ref, v_ref, g_ref, d_ref, r_ref, y_ref = refs[-7:]
    length = cur_ref.shape[1]
    lag = 4 * filt_ref.shape[1]
    block = length // 8
    keep = lag + 8
    for ref, m in ((k_ref, 1), (v_ref, 2)):
        ref[:keep, :] = prev_ref[m, prev_ref.shape[1] - keep :, :].astype(jnp.float32)
        ref[keep:, :] = cur_ref[m].astype(jnp.float32)

    def feature(ref, m, at, rows):
        return (
            taps_ref[m, 0:1, :] * ref[pl.ds(at, rows), :]
            + taps_ref[m, 1:2, :] * ref[pl.ds(at - 1, rows), :]
            + taps_ref[m, 2:3, :] * ref[pl.ds(at - 2, rows), :]
        )

    for r in range(0, lag + length, 128):
        gated = feature(k_ref, 1, r + 8, 128) * feature(v_ref, 2, r + 8, 128)
        g_ref[r : r + 128, :] = gated.astype(jnp.bfloat16).astype(jnp.float32)

    def spread(k):
        return g_ref[pl.ds(k, 8, stride=block), :]

    def split(step, carry):
        for n in range(4):
            n = step * 4 + n
            e = [spread(4 * n + q) for q in range(4)]
            pairs = ((e[0], e[2]), (e[1], e[3]), (e[0] + e[1], e[2] + e[3]))
            for w, (first, second) in enumerate(pairs):
                d_ref[3 * w, n] = first
                d_ref[3 * w + 1, n] = second
                d_ref[3 * w + 2, n] = first + second
        return carry

    lax.fori_loop(0, (block + lag) // 16, split, 0)
    count = block // 4 + 1
    base = lag // 4 - 1

    def short(n, carry):
        acc = [None] * count
        for q in range(lag // 4):
            weight = jnp.broadcast_to(filt_ref[n, pl.ds(q, 1), :], (8, 128))
            for i in range(count):
                term = weight * d_ref[n, base + i - q]
                acc[i] = term if q == 0 else acc[i] + term
        for i in range(count):
            r_ref[n, i] = acc[i]
        return carry

    lax.fori_loop(0, 9, short, 0)

    def before(w, m):
        return r_ref[3 * w + 2, m] - r_ref[3 * w, m] - r_ref[3 * w + 1, m]

    def exact(w, m):
        return r_ref[3 * w, m + 1] + r_ref[3 * w + 1, m]

    def join(step, late):
        for n in range(2):
            m = step * 2 + n
            for k, part in enumerate((exact, before)):
                even, odd, both = (part(w, m + k) for w in range(3))
                at = 4 * m + 2 * k
                y_ref[pl.ds(at, 8, stride=block), :] = even + late
                y_ref[pl.ds(at + 1, 8, stride=block), :] = both - even - odd
                late = odd
        return late

    lax.fori_loop(0, block // 8, join, before(1, 0))
    k_ref[:keep, :] = prev_ref[0, prev_ref.shape[1] - keep :, :].astype(jnp.float32)
    k_ref[keep:, :] = cur_ref[0].astype(jnp.float32)
    for r in range(0, length, 128):
        query = feature(k_ref, 0, keep + r, 128)
        out_ref[r : r + 128, :] = (query * y_ref[r : r + 128, :]).astype(jnp.bfloat16)


def medium(prev, prev_rows, prev_at, qkv, at, taps, filt, groups, start=0, onto=()):
    length, channels = ROWS, qkv.shape[2]
    lag = 4 * filt.shape[1]
    return pl.pallas_call(
        conv_kernel,
        out_shape=jax.ShapeDtypeStruct((length, channels), jnp.bfloat16),
        grid=(groups,),
        in_specs=[
            pl.BlockSpec((3, prev_rows, 128), lambda g: (0, prev_at, g + start)),
            pl.BlockSpec((3, length, 128), lambda g: (0, at, g + start)),
            pl.BlockSpec((3, 3, 128), lambda g: (0, 0, g + start)),
            pl.BlockSpec((9, lag // 4, 128), lambda g: (0, 0, g + start)),
        ]
        + [pl.BlockSpec(memory_space=pl.ANY)] * len(onto),
        out_specs=pl.BlockSpec((length, 128), lambda g: (0, g + start)),
        input_output_aliases={4: 0} if onto else {},
        scratch_shapes=[
            pltpu.VMEM((length + lag + 8, 128), jnp.float32),
            pltpu.VMEM((length + lag + 8, 128), jnp.float32),
            pltpu.VMEM((length + lag, 128), jnp.float32),
            pltpu.VMEM((9, (length // 8 + lag) // 4, 8, 128), jnp.float32),
            pltpu.VMEM((9, length // 32 + 1, 8, 128), jnp.float32),
            pltpu.VMEM((length, 128), jnp.float32),
        ],
        compiler_params=pltpu.CompilerParams(vmem_limit_bytes=16 << 20),
        name="medium",
    )(prev, qkv, taps, filt, *onto)


def split_taps(filters):
    f = filters.T.astype(jnp.float32).reshape(-1, 4, filters.shape[0])
    rows = []
    for first, second in ((f[:, 0], f[:, 2]), (f[:, 1], f[:, 3]), (f[:, 0] + f[:, 1], f[:, 2] + f[:, 3])):
        rows += [first, second, first + second]
    return jnp.stack(rows)


def featurize_into(edge_ref, lower_ref, upper_ref, at_upper, at_lower, taps_ref, m, x_ref):
    half = lower_ref.shape[1]
    x_ref[:8, :] = edge_ref[at_upper, edge_ref.shape[1] - 8 :, :].astype(jnp.float32)
    x_ref[8 : half + 8, :] = lower_ref[at_lower].astype(jnp.float32)
    x_ref[half + 8 :, :] = upper_ref[at_upper].astype(jnp.float32)

    def at(r, rows):
        return (
            taps_ref[m, 0:1, :] * x_ref[pl.ds(r + 8, rows), :]
            + taps_ref[m, 1:2, :] * x_ref[pl.ds(r + 7, rows), :]
            + taps_ref[m, 2:3, :] * x_ref[pl.ds(r + 6, rows), :]
        )

    return at


def scan_kernel(
    edge_ref, lower_ref, upper_ref, taps_ref, rates_ref, u_ref, starts_ref, end_ref, k_ref, v_ref, g_ref, p_ref
):
    poles = rates_ref.shape[0]
    length = 2 * lower_ref.shape[1]
    block = length // 8
    kf = featurize_into(edge_ref, lower_ref, upper_ref, 0, 0, taps_ref, 1, k_ref)
    vf = featurize_into(edge_ref, lower_ref, upper_ref, 1, 1, taps_ref, 2, v_ref)
    for r in range(0, length, 128):
        gated = (kf(r, 128) * vf(r, 128)).astype(jnp.bfloat16)
        g_ref[r : r + 128, :] = gated.astype(jnp.float32)
    for i in range(block):
        u_ref[i] = g_ref[pl.ds(i, 8, stride=block), :]
    pole = [jnp.broadcast_to(jnp.exp(-rates_ref[n : n + 1, :]), (8, 128)) for n in range(poles)]

    def advance(i, states):
        states = list(states)
        for s in range(4):
            u = u_ref[i * 4 + s]
            states = [p * a + u for p, a in zip(pole, states)]
        return tuple(states)

    zero = jnp.zeros((8, 128), jnp.float32)
    states = lax.fori_loop(0, block // 4, advance, (zero,) * poles)
    for n in range(poles):
        decay = jnp.exp(-rates_ref[n : n + 1, :] * block)
        p_ref[...] = states[n]
        run = jnp.zeros((1, 128), jnp.float32)
        for b in range(8):
            starts_ref[n, b : b + 1, :] = run
            run = decay * run + p_ref[b : b + 1, :]
        end_ref[n : n + 1, :] = run.astype(jnp.bfloat16)


def modal_scan(edge, lower, upper, taps, rates):
    half, channels = lower.shape[1:]
    length = 2 * half
    poles = rates.shape[0]
    line = lambda rows: pl.BlockSpec((rows, 128), lambda g: (0, g))
    cube = lambda rows: pl.BlockSpec((rows, 8, 128), lambda g: (0, 0, g))
    return pl.pallas_call(
        scan_kernel,
        out_shape=(
            jax.ShapeDtypeStruct((length // 8, 8, channels), jnp.float32),
            jax.ShapeDtypeStruct((poles, 8, channels), jnp.float32),
            jax.ShapeDtypeStruct((poles, channels), jnp.bfloat16),
        ),
        grid=(channels // 128,),
        in_specs=[
            pl.BlockSpec((2, 16, 128), lambda g: (0, 0, g)),
            pl.BlockSpec((2, half, 128), lambda g: (0, 0, g)),
            pl.BlockSpec((2, half, 128), lambda g: (0, 0, g)),
            pl.BlockSpec((3, 3, 128), lambda g: (0, 0, g)),
            line(poles),
        ],
        out_specs=(cube(length // 8), cube(poles), line(poles)),
        scratch_shapes=[
            pltpu.VMEM((length + 8, 128), jnp.float32),
            pltpu.VMEM((length + 8, 128), jnp.float32),
            pltpu.VMEM((length, 128), jnp.float32),
            pltpu.VMEM((8, 128), jnp.float32),
        ],
        compiler_params=pltpu.CompilerParams(vmem_limit_bytes=16 << 20),
        name="modal_scan",
    )(edge, lower, upper, taps, rates)


def finish_kernel(
    edge_ref, lower_ref, upper_ref, taps_ref, rates_ref, residues_ref, skip_ref, u_ref, starts_ref, enter_ref, out_ref, q_ref, y_ref
):
    poles = rates_ref.shape[0]
    length = 2 * lower_ref.shape[1]
    block = length // 8
    pole = [jnp.broadcast_to(jnp.exp(-rates_ref[n : n + 1, :]), (8, 128)) for n in range(poles)]
    weight = [jnp.broadcast_to(residues_ref[n : n + 1, :], (8, 128)) for n in range(poles)]
    skip = jnp.broadcast_to(skip_ref[...], (8, 128))
    place = lax.broadcasted_iota(jnp.int32, (8, 128), 0).astype(jnp.float32) * block
    states = tuple(
        starts_ref[n] + jnp.exp(-rates_ref[n : n + 1, :] * place) * enter_ref[n : n + 1, :]
        for n in range(poles)
    )

    def advance(j, states):
        for s in range(4):
            i = j * 4 + s
            u = u_ref[i]
            states = [p * a + u for p, a in zip(pole, states)]
            parts = [w * a for w, a in zip(weight, states)] + [skip * u]
            while len(parts) > 1:
                parts = [a + b for a, b in zip(parts[::2], parts[1::2])] + parts[len(parts) & ~1 :]
            y_ref[pl.ds(i, 8, stride=block), :] = parts[0]
        return tuple(states)

    lax.fori_loop(0, block // 4, advance, states)
    qf = featurize_into(edge_ref, lower_ref, upper_ref, 0, 0, taps_ref, 0, q_ref)
    for r in range(0, length, 128):
        out_ref[r : r + 128, :] = (qf(r, 128) * y_ref[r : r + 128, :]).astype(jnp.bfloat16)


def modal_finish(edge, lower, upper, taps, rates, residues, skip, u, starts, enter):
    half, channels = lower.shape[1:]
    length = 2 * half
    poles = rates.shape[0]
    line = lambda rows: pl.BlockSpec((rows, 128), lambda g: (0, g))
    cube = lambda rows: pl.BlockSpec((rows, 8, 128), lambda g: (0, 0, g))
    return pl.pallas_call(
        finish_kernel,
        out_shape=jax.ShapeDtypeStruct((length, channels), jnp.bfloat16),
        grid=(channels // 128,),
        in_specs=[
            pl.BlockSpec((1, 16, 128), lambda g: (0, 0, g)),
            pl.BlockSpec((1, half, 128), lambda g: (0, 0, g)),
            pl.BlockSpec((1, half, 128), lambda g: (0, 0, g)),
            pl.BlockSpec((3, 3, 128), lambda g: (0, 0, g)),
            line(poles),
            line(poles),
            line(1),
            cube(length // 8),
            cube(poles),
            line(poles),
        ],
        out_specs=line(length),
        scratch_shapes=[
            pltpu.VMEM((length + 8, 128), jnp.float32),
            pltpu.VMEM((length, 128), jnp.float32),
        ],
        compiler_params=pltpu.CompilerParams(vmem_limit_bytes=16 << 20),
        name="modal_finish",
    )(edge, lower, upper, taps, rates, residues, skip.reshape(1, channels), u, starts, enter)


D = 4096
EPSILON = 1e-05
ROWS = 512
HALF = 256
EXTRA = 16


def x_pairs(d):
    return [(c, c // 4 * 4 + (c + d) % 4) for c in range(16)]


def y_pairs(d):
    return [(c, (c + 4 * d) % 16) for c in range(16)]


def z_pairs(d):
    return [(t, (t + 2 * d) % 8) for t in range(8)]


def core_pairs():
    return [(t, t ^ 1) for t in range(8)]


def ring(a, axis, pairs):
    return [a] + [lax.ppermute(a, axis, pairs(-d)) for d in (1, 2, 3)]


def plane_gather(a, first, second):
    pieces = ring(a, "ctx", first)
    return ring(jnp.stack(pieces), "ctx", second)


def near_gather(a):
    pieces = ring(a, "tp", z_pairs)
    return (*pieces, *[lax.ppermute(p, "tp", core_pairs()) for p in pieces])


def token_gather(a):
    after = lax.ppermute(a, "tp", z_pairs(-1))
    before = lax.ppermute(a, "tp", z_pairs(1))
    low = lax.ppermute(after[:HALF], "tp", z_pairs(-1))
    high = lax.ppermute(before[HALF:], "tp", z_pairs(1))
    pieces = (a, after, low, high, before)
    return (*pieces, *[lax.ppermute(p, "tp", core_pairs()) for p in pieces])


def mix_kernel(place_ref, *refs):
    acts, west, south, refs = refs[:8], refs[8:12], refs[12:16], refs[16:]
    residual_ref, gain_ref, out_ref, send_ref, act_ref = refs
    y, x, z, core = (place_ref[n] for n in range(4))
    rows = act_ref.shape[1]
    for s in range(2):
        for dz in range(4):
            at = (z + dz) % 4 * 4 + (core ^ s) * 2
            for h in range(2):
                act_ref[at + h] = acts[4 * s + dz][:, h * 256 : h * 256 + 256]
    squares = jnp.zeros((EXTRA, rows), jnp.float32)
    for side, weights in enumerate((west, south)):
        total = jnp.zeros((rows, 256), jnp.float32)
        for outer in range(4):
            left, right = [], []
            for inner in range(4):
                dy, dx = (outer, inner) if side == 0 else (inner, outer)
                left.append(act_ref[(y + dy) % 4 * 4 + (x + dx) % 4])
                right.append(weights[outer][inner])
            total = total + jnp.dot(
                jnp.concatenate(left, axis=1),
                jnp.concatenate(right, axis=0),
                preferred_element_type=jnp.float32,
            )
        lanes = slice(side * 256, side * 256 + 256)
        hidden = (residual_ref[:, lanes].astype(jnp.float32) + total).astype(jnp.bfloat16)
        out_ref[:, lanes] = hidden
        wide = hidden.astype(jnp.float32)
        gain = gain_ref[:, lanes].astype(jnp.float32)
        send_ref[:rows, lanes] = (wide * gain).astype(jnp.bfloat16)
        squares = squares + lax.dot_general(
            jnp.ones((EXTRA, 256), jnp.float32),
            wide * wide,
            (((1,), (1,)), ((), ())),
            precision=lax.Precision.HIGHEST,
            preferred_element_type=jnp.float32,
        )
    high = squares.astype(jnp.bfloat16)
    rest = squares - high.astype(jnp.float32)
    middle = rest.astype(jnp.bfloat16)
    low = (rest - middle.astype(jnp.float32)).astype(jnp.bfloat16)
    row = lax.broadcasted_iota(jnp.int32, squares.shape, 0)
    terms = [a.astype(jnp.float32) for a in (high, middle, low)]
    terms = jnp.where(row == 0, terms[0], jnp.where(row == 1, terms[1], terms[2]))
    send_ref[rows:, :] = terms.astype(jnp.bfloat16)


def mix(place, acts, west, south, residual, gain, at):
    rows, channels = ROWS, acts[0].shape[1]
    whole = lambda a: pl.BlockSpec(a.shape, lambda j, _: (0,) * a.ndim)
    return pl.pallas_call(
        mix_kernel,
        out_shape=(
            jax.ShapeDtypeStruct((rows, channels), jnp.bfloat16),
            jax.ShapeDtypeStruct((rows + EXTRA, channels), jnp.bfloat16),
        ),
        grid_spec=pltpu.PrefetchScalarGridSpec(
            num_scalar_prefetch=1,
            grid=(1,),
            in_specs=[whole(a) for a in (*acts, *west, *south)]
            + [
                pl.BlockSpec((rows, channels), lambda j, _: (at, 0)),
                pl.BlockSpec((1, channels), lambda j, _: (0, 0)),
            ],
            out_specs=(
                pl.BlockSpec((rows, channels), lambda j, _: (0, 0)),
                pl.BlockSpec((rows + EXTRA, channels), lambda j, _: (0, 0)),
            ),
            scratch_shapes=[pltpu.VMEM((16, rows, 256), jnp.bfloat16)],
        ),
        compiler_params=pltpu.CompilerParams(vmem_limit_bytes=40 << 20),
        name="mix",
    )(place, *acts, *west, *south, residual, gain.reshape(1, channels))


def project_kernel(place_ref, *refs):
    acts, (weight_ref, out_ref, scale_ref) = refs[:10], refs[10:]
    z, core = place_ref[2], place_ref[3]
    rows = out_ref.shape[1]

    @pl.when((pl.program_id(0) == 0) & (pl.program_id(1) == 0))
    def _():
        total = jnp.zeros((1, rows), jnp.float32)
        for ref in acts[:2] + acts[3:7] + acts[8:]:
            terms = ref[ref.shape[0] - EXTRA :, :].astype(jnp.float32)
            total = total + (terms[0:1, :] + terms[1:2, :] + terms[2:3, :])
        scale = lax.rsqrt(total / D + EPSILON)
        scale_ref[...] = jnp.transpose(jnp.broadcast_to(scale, (128, rows)))

    left, right = [], []
    for s in range(2):
        for dz in range(4):
            if dz == 2:
                parts = [acts[5 * s + 2][...], acts[5 * s + 3][:HALF, :]]
                left.append(jnp.concatenate(parts, axis=0))
            else:
                left.append(acts[5 * s + (0, 1, 2, 4)[dz]][:rows, :])
            at = (z + dz) % 4 * 4 + (core ^ s) * 2
            right += [weight_ref[at, 0], weight_ref[at + 1, 0]]
    total = jnp.dot(
        jnp.concatenate(left, axis=1),
        jnp.concatenate(right, axis=0),
        preferred_element_type=jnp.float32,
    )
    scale = jnp.concatenate([scale_ref[...], scale_ref[...]], axis=1)
    out_ref[0] = (total * scale).astype(jnp.bfloat16)


def project(place, acts, weight, start, count):
    rows, channels = ROWS, acts[0].shape[1]
    return pl.pallas_call(
        project_kernel,
        out_shape=jax.ShapeDtypeStruct((count, rows, channels), jnp.bfloat16),
        grid_spec=pltpu.PrefetchScalarGridSpec(
            num_scalar_prefetch=1,
            grid=(count, channels // 256),
            in_specs=[pl.BlockSpec(a.shape, lambda m, n, _: (0, 0)) for a in acts]
            + [pl.BlockSpec((16, 1, 256, 256), lambda m, n, _: (0, m + start, 0, n))],
            out_specs=pl.BlockSpec((1, rows, 256), lambda m, n, _: (m, 0, n)),
            scratch_shapes=[pltpu.VMEM((rows, 128), jnp.float32)],
        ),
        name="project",
    )(place, *acts, weight)


def on_device(
    qkv_first,
    short_first,
    medium_filter,
    out_weight,
    residual_in,
    norm_gain,
    in_weight,
    short_second,
    rates,
    residues,
    skip_gain,
):
    length = qkv_first.shape[1]
    c = lax.axis_index("ctx")
    t = lax.axis_index("tp")
    x, y, core, z = c % 4, c // 4, t % 2, t // 2
    place = jnp.stack([y, x, z, core]).astype(jnp.int32)
    ahead = [(i, i + 1) for i in range(15)]

    packed = out_weight.reshape(2, 256, 256)
    odd = c % 2
    turned = []
    for k in range(2):
        pairs = []
        for cc in range(16):
            for tt in range(8):
                to = (2 * tt + (cc + k) % 2, cc // 2)
                pairs.append((cc * 8 + tt, to[0] * 8 + to[1]))
        mine = lax.dynamic_index_in_dim(packed, (odd + k) % 2, 0, False)
        turned.append(lax.ppermute(mine, ("ctx", "tp"), pairs))
    rim = lax.ppermute(qkv_first[:, length - HALO :], "ctx", ahead)
    first = jnp.where(odd == 0, turned[0], turned[1])
    second = jnp.where(odd == 0, turned[1], turned[0])
    weight = lax.all_gather(in_weight[1:], "ctx")
    query_weight = lax.all_gather(in_weight[:1], "ctx")
    out_west = plane_gather(first, x_pairs, y_pairs)
    out_south = plane_gather(second, y_pairs, x_pairs)

    filt = split_taps(medium_filter)
    upper = medium(qkv_first, 256, 1, qkv_first, 1, short_first, filt, 2)
    upper = medium(qkv_first, 256, 1, qkv_first, 1, short_first, filt, 2, 2, (upper,))
    upper_pieces = near_gather(upper)
    lower = medium(rim, HALO, 0, qkv_first, 0, short_first, filt, 4)
    lower_pieces = near_gather(lower)
    hidden_upper, send_upper = mix(
        place, upper_pieces, out_west, out_south, residual_in, norm_gain, 1
    )
    send_upper = token_gather(send_upper)
    hidden_lower, send_lower = mix(
        place, lower_pieces, out_west, out_south, residual_in, norm_gain, 0
    )
    send_lower = token_gather(send_lower)
    hidden = jnp.concatenate([hidden_lower, hidden_upper], axis=0)
    kv_upper = project(place, send_upper, weight, 0, 2)
    edge = lax.ppermute(kv_upper[:, ROWS - 16 :], "ctx", ahead)
    kv_lower = project(place, send_lower, weight, 0, 2)
    u, starts, end = modal_scan(edge, kv_lower, kv_upper, short_second, rates)
    log_decay = -rates * length

    def decay(k):
        return jnp.exp(log_decay * k.astype(jnp.float32))

    along = ring(end, "ctx", x_pairs)
    row = jnp.zeros_like(rates)
    enter = jnp.zeros_like(rates)
    for d, e in enumerate(along):
        at = (x + d) % 4
        wide = e.astype(jnp.float32)
        row = row + decay(3 - at) * wide
        enter = enter + jnp.where(at < x, decay(jnp.maximum(x - 1 - at, 0)), 0.0) * wide
    row = row.astype(jnp.bfloat16)
    up = ring(row, "ctx", y_pairs)
    for d in (1, 2, 3):
        e = up[d]
        at = (y + d) % 4
        enter = enter + jnp.where(
            at < y, decay(x + 4 * jnp.maximum(y - 1 - at, 0)), 0.0
        ) * e.astype(jnp.float32)
    q_upper = project(place, send_upper, query_weight, 0, 1)
    edge = lax.ppermute(q_upper[:, ROWS - 16 :], "ctx", ahead)
    q_lower = project(place, send_lower, query_weight, 0, 1)
    mixed = modal_finish(
        edge, q_lower, q_upper, short_second, rates, residues, skip_gain, u, starts, enter
    )
    return (hidden, mixed)


def solution(mesh):
    placed = (
        P(None, "ctx", "tp"),
        P(None, None, "tp"),
        P("tp", None),
        P("tp", "ctx"),
        P("ctx", "tp"),
        P("tp"),
        P(None, "ctx", "tp"),
        P(None, None, "tp"),
        P(None, "tp"),
        P(None, "tp"),
        P("tp"),
    )
    return jax.shard_map(
        on_device,
        mesh=mesh,
        in_specs=placed,
        out_specs=(P("ctx", "tp"), P("ctx", "tp")),
        check_vma=False,
    )
```

```python
import jax
import jax.numpy as jnp
from jax import lax
from jax.experimental import pallas as pl
from jax.experimental.pallas import tpu as pltpu
from jax.sharding import PartitionSpec as P

HALO = 144


def conv_kernel(prev_ref, cur_ref, taps_ref, filt_ref, *refs):
    out_ref, k_ref, v_ref, g_ref, d_ref, r_ref, y_ref = refs[-7:]
    length = cur_ref.shape[1]
    lag = 4 * filt_ref.shape[1]
    block = length // 8
    keep = lag + 8
    for ref, m in ((k_ref, 1), (v_ref, 2)):
        ref[:keep, :] = prev_ref[m, prev_ref.shape[1] - keep :, :].astype(jnp.float32)
        ref[keep:, :] = cur_ref[m].astype(jnp.float32)

    def feature(ref, m, at, rows):
        return (
            taps_ref[m, 0:1, :] * ref[pl.ds(at, rows), :]
            + taps_ref[m, 1:2, :] * ref[pl.ds(at - 1, rows), :]
            + taps_ref[m, 2:3, :] * ref[pl.ds(at - 2, rows), :]
        )

    for r in range(0, lag + length, 128):
        gated = feature(k_ref, 1, r + 8, 128) * feature(v_ref, 2, r + 8, 128)
        g_ref[r : r + 128, :] = gated.astype(jnp.bfloat16).astype(jnp.float32)

    def spread(k):
        return g_ref[pl.ds(k, 8, stride=block), :]

    def split(step, carry):
        for n in range(4):
            n = step * 4 + n
            e = [spread(4 * n + q) for q in range(4)]
            pairs = ((e[0], e[2]), (e[1], e[3]), (e[0] + e[1], e[2] + e[3]))
            for w, (first, second) in enumerate(pairs):
                d_ref[3 * w, n] = first
                d_ref[3 * w + 1, n] = second
                d_ref[3 * w + 2, n] = first + second
        return carry

    lax.fori_loop(0, (block + lag) // 16, split, 0)
    count = block // 4 + 1
    base = lag // 4 - 1

    def short(n, carry):
        acc = [None] * count
        for q in range(lag // 4):
            weight = jnp.broadcast_to(filt_ref[n, pl.ds(q, 1), :], (8, 128))
            for i in range(count):
                term = weight * d_ref[n, base + i - q]
                acc[i] = term if q == 0 else acc[i] + term
        for i in range(count):
            r_ref[n, i] = acc[i]
        return carry

    lax.fori_loop(0, 9, short, 0)

    def before(w, m):
        return r_ref[3 * w + 2, m] - r_ref[3 * w, m] - r_ref[3 * w + 1, m]

    def exact(w, m):
        return r_ref[3 * w, m + 1] + r_ref[3 * w + 1, m]

    def join(step, late):
        for n in range(2):
            m = step * 2 + n
            for k, part in enumerate((exact, before)):
                even, odd, both = (part(w, m + k) for w in range(3))
                at = 4 * m + 2 * k
                y_ref[pl.ds(at, 8, stride=block), :] = even + late
                y_ref[pl.ds(at + 1, 8, stride=block), :] = both - even - odd
                late = odd
        return late

    lax.fori_loop(0, block // 8, join, before(1, 0))
    k_ref[:keep, :] = prev_ref[0, prev_ref.shape[1] - keep :, :].astype(jnp.float32)
    k_ref[keep:, :] = cur_ref[0].astype(jnp.float32)
    for r in range(0, length, 128):
        query = feature(k_ref, 0, keep + r, 128)
        out_ref[r : r + 128, :] = (query * y_ref[r : r + 128, :]).astype(jnp.bfloat16)


def medium(prev, prev_rows, prev_at, qkv, at, taps, filt, groups, start=0, onto=()):
    length, channels = ROWS, qkv.shape[2]
    lag = 4 * filt.shape[1]
    return pl.pallas_call(
        conv_kernel,
        out_shape=jax.ShapeDtypeStruct((length, channels), jnp.bfloat16),
        grid=(groups,),
        in_specs=[
            pl.BlockSpec((3, prev_rows, 128), lambda g: (0, prev_at, g + start)),
            pl.BlockSpec((3, length, 128), lambda g: (0, at, g + start)),
            pl.BlockSpec((3, 3, 128), lambda g: (0, 0, g + start)),
            pl.BlockSpec((9, lag // 4, 128), lambda g: (0, 0, g + start)),
        ]
        + [pl.BlockSpec(memory_space=pl.ANY)] * len(onto),
        out_specs=pl.BlockSpec((length, 128), lambda g: (0, g + start)),
        input_output_aliases={4: 0} if onto else {},
        scratch_shapes=[
            pltpu.VMEM((length + lag + 8, 128), jnp.float32),
            pltpu.VMEM((length + lag + 8, 128), jnp.float32),
            pltpu.VMEM((length + lag, 128), jnp.float32),
            pltpu.VMEM((9, (length // 8 + lag) // 4, 8, 128), jnp.float32),
            pltpu.VMEM((9, length // 32 + 1, 8, 128), jnp.float32),
            pltpu.VMEM((length, 128), jnp.float32),
        ],
        compiler_params=pltpu.CompilerParams(vmem_limit_bytes=16 << 20),
        name="medium",
    )(prev, qkv, taps, filt, *onto)


def split_taps(filters):
    f = filters.T.astype(jnp.float32).reshape(-1, 4, filters.shape[0])
    rows = []
    for first, second in ((f[:, 0], f[:, 2]), (f[:, 1], f[:, 3]), (f[:, 0] + f[:, 1], f[:, 2] + f[:, 3])):
        rows += [first, second, first + second]
    return jnp.stack(rows)


def featurize_into(edge_ref, lower_ref, upper_ref, at_upper, at_lower, taps_ref, m, x_ref):
    half = lower_ref.shape[1]
    x_ref[:8, :] = edge_ref[at_upper, edge_ref.shape[1] - 8 :, :].astype(jnp.float32)
    x_ref[8 : half + 8, :] = lower_ref[at_lower].astype(jnp.float32)
    x_ref[half + 8 :, :] = upper_ref[at_upper].astype(jnp.float32)

    def at(r, rows):
        return (
            taps_ref[m, 0:1, :] * x_ref[pl.ds(r + 8, rows), :]
            + taps_ref[m, 1:2, :] * x_ref[pl.ds(r + 7, rows), :]
            + taps_ref[m, 2:3, :] * x_ref[pl.ds(r + 6, rows), :]
        )

    return at


def scan_kernel(
    edge_ref, lower_ref, upper_ref, taps_ref, rates_ref, u_ref, starts_ref, end_ref, k_ref, v_ref, g_ref, p_ref
):
    poles = rates_ref.shape[0]
    length = 2 * lower_ref.shape[1]
    block = length // 8
    kf = featurize_into(edge_ref, lower_ref, upper_ref, 0, 0, taps_ref, 1, k_ref)
    vf = featurize_into(edge_ref, lower_ref, upper_ref, 1, 1, taps_ref, 2, v_ref)
    for r in range(0, length, 128):
        gated = (kf(r, 128) * vf(r, 128)).astype(jnp.bfloat16)
        g_ref[r : r + 128, :] = gated.astype(jnp.float32)
    for i in range(block):
        u_ref[i] = g_ref[pl.ds(i, 8, stride=block), :]
    pole = [jnp.broadcast_to(jnp.exp(-rates_ref[n : n + 1, :]), (8, 128)) for n in range(poles)]

    def advance(i, states):
        states = list(states)
        for s in range(4):
            u = u_ref[i * 4 + s]
            states = [p * a + u for p, a in zip(pole, states)]
        return tuple(states)

    zero = jnp.zeros((8, 128), jnp.float32)
    states = lax.fori_loop(0, block // 4, advance, (zero,) * poles)
    for n in range(poles):
        decay = jnp.exp(-rates_ref[n : n + 1, :] * block)
        p_ref[...] = states[n]
        run = jnp.zeros((1, 128), jnp.float32)
        for b in range(8):
            starts_ref[n, b : b + 1, :] = run
            run = decay * run + p_ref[b : b + 1, :]
        end_ref[n : n + 1, :] = run.astype(jnp.bfloat16)


def modal_scan(edge, lower, upper, taps, rates):
    half, channels = lower.shape[1:]
    length = 2 * half
    poles = rates.shape[0]
    line = lambda rows: pl.BlockSpec((rows, 128), lambda g: (0, g))
    cube = lambda rows: pl.BlockSpec((rows, 8, 128), lambda g: (0, 0, g))
    return pl.pallas_call(
        scan_kernel,
        out_shape=(
            jax.ShapeDtypeStruct((length // 8, 8, channels), jnp.float32),
            jax.ShapeDtypeStruct((poles, 8, channels), jnp.float32),
            jax.ShapeDtypeStruct((poles, channels), jnp.bfloat16),
        ),
        grid=(channels // 128,),
        in_specs=[
            pl.BlockSpec((2, 16, 128), lambda g: (0, 0, g)),
            pl.BlockSpec((2, half, 128), lambda g: (0, 0, g)),
            pl.BlockSpec((2, half, 128), lambda g: (0, 0, g)),
            pl.BlockSpec((3, 3, 128), lambda g: (0, 0, g)),
            line(poles),
        ],
        out_specs=(cube(length // 8), cube(poles), line(poles)),
        scratch_shapes=[
            pltpu.VMEM((length + 8, 128), jnp.float32),
            pltpu.VMEM((length + 8, 128), jnp.float32),
            pltpu.VMEM((length, 128), jnp.float32),
            pltpu.VMEM((8, 128), jnp.float32),
        ],
        compiler_params=pltpu.CompilerParams(vmem_limit_bytes=16 << 20),
        name="modal_scan",
    )(edge, lower, upper, taps, rates)


def finish_kernel(
    edge_ref, lower_ref, upper_ref, taps_ref, rates_ref, residues_ref, skip_ref, u_ref, starts_ref, enter_ref, out_ref, q_ref, y_ref
):
    poles = rates_ref.shape[0]
    length = 2 * lower_ref.shape[1]
    block = length // 8
    pole = [jnp.broadcast_to(jnp.exp(-rates_ref[n : n + 1, :]), (8, 128)) for n in range(poles)]
    weight = [jnp.broadcast_to(residues_ref[n : n + 1, :], (8, 128)) for n in range(poles)]
    skip = jnp.broadcast_to(skip_ref[...], (8, 128))
    place = lax.broadcasted_iota(jnp.int32, (8, 128), 0).astype(jnp.float32) * block
    states = tuple(
        starts_ref[n] + jnp.exp(-rates_ref[n : n + 1, :] * place) * enter_ref[n : n + 1, :]
        for n in range(poles)
    )

    def advance(j, states):
        for s in range(4):
            i = j * 4 + s
            u = u_ref[i]
            states = [p * a + u for p, a in zip(pole, states)]
            parts = [w * a for w, a in zip(weight, states)] + [skip * u]
            while len(parts) > 1:
                parts = [a + b for a, b in zip(parts[::2], parts[1::2])] + parts[len(parts) & ~1 :]
            y_ref[pl.ds(i, 8, stride=block), :] = parts[0]
        return tuple(states)

    lax.fori_loop(0, block // 4, advance, states)
    qf = featurize_into(edge_ref, lower_ref, upper_ref, 0, 0, taps_ref, 0, q_ref)
    for r in range(0, length, 128):
        out_ref[r : r + 128, :] = (qf(r, 128) * y_ref[r : r + 128, :]).astype(jnp.bfloat16)


def modal_finish(edge, lower, upper, taps, rates, residues, skip, u, starts, enter):
    half, channels = lower.shape[1:]
    length = 2 * half
    poles = rates.shape[0]
    line = lambda rows: pl.BlockSpec((rows, 128), lambda g: (0, g))
    cube = lambda rows: pl.BlockSpec((rows, 8, 128), lambda g: (0, 0, g))
    return pl.pallas_call(
        finish_kernel,
        out_shape=jax.ShapeDtypeStruct((length, channels), jnp.bfloat16),
        grid=(channels // 128,),
        in_specs=[
            pl.BlockSpec((1, 16, 128), lambda g: (0, 0, g)),
            pl.BlockSpec((1, half, 128), lambda g: (0, 0, g)),
            pl.BlockSpec((1, half, 128), lambda g: (0, 0, g)),
            pl.BlockSpec((3, 3, 128), lambda g: (0, 0, g)),
            line(poles),
            line(poles),
            line(1),
            cube(length // 8),
            cube(poles),
            line(poles),
        ],
        out_specs=line(length),
        scratch_shapes=[
            pltpu.VMEM((length + 8, 128), jnp.float32),
            pltpu.VMEM((length, 128), jnp.float32),
        ],
        compiler_params=pltpu.CompilerParams(vmem_limit_bytes=16 << 20),
        name="modal_finish",
    )(edge, lower, upper, taps, rates, residues, skip.reshape(1, channels), u, starts, enter)


D = 4096
EPSILON = 1e-05
ROWS = 512
HALF = 256
EXTRA = 16


def x_pairs(d):
    return [(c, c // 4 * 4 + (c + d) % 4) for c in range(16)]


def y_pairs(d):
    return [(c, (c + 4 * d) % 16) for c in range(16)]


def z_pairs(d):
    return [(t, (t + 2 * d) % 8) for t in range(8)]


def core_pairs():
    return [(t, t ^ 1) for t in range(8)]


def ring(a, axis, pairs):
    return [a] + [lax.ppermute(a, axis, pairs(-d)) for d in (1, 2, 3)]


def plane_gather(a, first, second):
    pieces = ring(a, "ctx", first)
    return ring(jnp.stack(pieces), "ctx", second)


def near_gather(a):
    pieces = ring(a, "tp", z_pairs)
    return (*pieces, *[lax.ppermute(p, "tp", core_pairs()) for p in pieces])


def token_gather(a):
    after = lax.ppermute(a, "tp", z_pairs(-1))
    before = lax.ppermute(a, "tp", z_pairs(1))
    low = lax.ppermute(after[:HALF], "tp", z_pairs(-1))
    high = lax.ppermute(before[HALF:], "tp", z_pairs(1))
    pieces = (a, after, low, high, before)
    return (*pieces, *[lax.ppermute(p, "tp", core_pairs()) for p in pieces])


def mix_kernel(place_ref, *refs):
    acts, west, south, refs = refs[:8], refs[8:12], refs[12:16], refs[16:]
    residual_ref, gain_ref, out_ref, send_ref, act_ref = refs
    y, x, z, core = (place_ref[n] for n in range(4))
    rows = act_ref.shape[1]
    for s in range(2):
        for dz in range(4):
            at = (z + dz) % 4 * 4 + (core ^ s) * 2
            for h in range(2):
                act_ref[at + h] = acts[4 * s + dz][:, h * 256 : h * 256 + 256]
    squares = jnp.zeros((EXTRA, rows), jnp.float32)
    for side, weights in enumerate((west, south)):
        total = jnp.zeros((rows, 256), jnp.float32)
        for outer in range(4):
            left, right = [], []
            for inner in range(4):
                dy, dx = (outer, inner) if side == 0 else (inner, outer)
                left.append(act_ref[(y + dy) % 4 * 4 + (x + dx) % 4])
                right.append(weights[outer][inner])
            total = total + jnp.dot(
                jnp.concatenate(left, axis=1),
                jnp.concatenate(right, axis=0),
                preferred_element_type=jnp.float32,
            )
        lanes = slice(side * 256, side * 256 + 256)
        hidden = (residual_ref[:, lanes].astype(jnp.float32) + total).astype(jnp.bfloat16)
        out_ref[:, lanes] = hidden
        wide = hidden.astype(jnp.float32)
        gain = gain_ref[:, lanes].astype(jnp.float32)
        send_ref[:rows, lanes] = (wide * gain).astype(jnp.bfloat16)
        squares = squares + lax.dot_general(
            jnp.ones((EXTRA, 256), jnp.float32),
            wide * wide,
            (((1,), (1,)), ((), ())),
            precision=lax.Precision.HIGHEST,
            preferred_element_type=jnp.float32,
        )
    high = squares.astype(jnp.bfloat16)
    rest = squares - high.astype(jnp.float32)
    middle = rest.astype(jnp.bfloat16)
    low = (rest - middle.astype(jnp.float32)).astype(jnp.bfloat16)
    row = lax.broadcasted_iota(jnp.int32, squares.shape, 0)
    terms = [a.astype(jnp.float32) for a in (high, middle, low)]
    terms = jnp.where(row == 0, terms[0], jnp.where(row == 1, terms[1], terms[2]))
    send_ref[rows:, :] = terms.astype(jnp.bfloat16)


def mix(place, acts, west, south, residual, gain, at):
    rows, channels = ROWS, acts[0].shape[1]
    whole = lambda a: pl.BlockSpec(a.shape, lambda j, _: (0,) * a.ndim)
    return pl.pallas_call(
        mix_kernel,
        out_shape=(
            jax.ShapeDtypeStruct((rows, channels), jnp.bfloat16),
            jax.ShapeDtypeStruct((rows + EXTRA, channels), jnp.bfloat16),
        ),
        grid_spec=pltpu.PrefetchScalarGridSpec(
            num_scalar_prefetch=1,
            grid=(1,),
            in_specs=[whole(a) for a in (*acts, *west, *south)]
            + [
                pl.BlockSpec((rows, channels), lambda j, _: (at, 0)),
                pl.BlockSpec((1, channels), lambda j, _: (0, 0)),
            ],
            out_specs=(
                pl.BlockSpec((rows, channels), lambda j, _: (0, 0)),
                pl.BlockSpec((rows + EXTRA, channels), lambda j, _: (0, 0)),
            ),
            scratch_shapes=[pltpu.VMEM((16, rows, 256), jnp.bfloat16)],
        ),
        compiler_params=pltpu.CompilerParams(vmem_limit_bytes=40 << 20),
        name="mix",
    )(place, *acts, *west, *south, residual, gain.reshape(1, channels))


def project_kernel(place_ref, *refs):
    acts, (weight_ref, out_ref, scale_ref) = refs[:10], refs[10:]
    z, core = place_ref[2], place_ref[3]
    rows = out_ref.shape[1]

    @pl.when((pl.program_id(0) == 0) & (pl.program_id(1) == 0))
    def _():
        total = jnp.zeros((1, rows), jnp.float32)
        for ref in acts[:2] + acts[3:7] + acts[8:]:
            terms = ref[ref.shape[0] - EXTRA :, :].astype(jnp.float32)
            total = total + (terms[0:1, :] + terms[1:2, :] + terms[2:3, :])
        scale = lax.rsqrt(total / D + EPSILON)
        scale_ref[...] = jnp.transpose(jnp.broadcast_to(scale, (128, rows)))

    left, right = [], []
    for s in range(2):
        for dz in range(4):
            if dz == 2:
                parts = [acts[5 * s + 2][...], acts[5 * s + 3][:HALF, :]]
                left.append(jnp.concatenate(parts, axis=0))
            else:
                left.append(acts[5 * s + (0, 1, 2, 4)[dz]][:rows, :])
            at = (z + dz) % 4 * 4 + (core ^ s) * 2
            right += [weight_ref[at, 0], weight_ref[at + 1, 0]]
    total = jnp.dot(
        jnp.concatenate(left, axis=1),
        jnp.concatenate(right, axis=0),
        preferred_element_type=jnp.float32,
    )
    scale = jnp.concatenate([scale_ref[...], scale_ref[...]], axis=1)
    out_ref[0] = (total * scale).astype(jnp.bfloat16)


def project(place, acts, weight, start, count):
    rows, channels = ROWS, acts[0].shape[1]
    return pl.pallas_call(
        project_kernel,
        out_shape=jax.ShapeDtypeStruct((count, rows, channels), jnp.bfloat16),
        grid_spec=pltpu.PrefetchScalarGridSpec(
            num_scalar_prefetch=1,
            grid=(count, channels // 256),
            in_specs=[pl.BlockSpec(a.shape, lambda m, n, _: (0, 0)) for a in acts]
            + [pl.BlockSpec((16, 1, 256, 256), lambda m, n, _: (0, m + start, 0, n))],
            out_specs=pl.BlockSpec((1, rows, 256), lambda m, n, _: (m, 0, n)),
            scratch_shapes=[pltpu.VMEM((rows, 128), jnp.float32)],
        ),
        name="project",
    )(place, *acts, weight)


def on_device(
    qkv_first,
    short_first,
    medium_filter,
    out_weight,
    residual_in,
    norm_gain,
    in_weight,
    short_second,
    rates,
    residues,
    skip_gain,
):
    length = qkv_first.shape[1]
    c = lax.axis_index("ctx")
    t = lax.axis_index("tp")
    x, y, core, z = c % 4, c // 4, t % 2, t // 2
    place = jnp.stack([y, x, z, core]).astype(jnp.int32)
    ahead = [(i, i + 1) for i in range(15)]

    packed = out_weight.reshape(2, 256, 256)
    odd = c % 2
    turned = []
    for k in range(2):
        pairs = []
        for cc in range(16):
            for tt in range(8):
                to = (2 * tt + (cc + k) % 2, cc // 2)
                pairs.append((cc * 8 + tt, to[0] * 8 + to[1]))
        mine = lax.dynamic_index_in_dim(packed, (odd + k) % 2, 0, False)
        turned.append(lax.ppermute(mine, ("ctx", "tp"), pairs))
    rim = lax.ppermute(qkv_first[:, length - HALO :], "ctx", ahead)
    first = jnp.where(odd == 0, turned[0], turned[1])
    second = jnp.where(odd == 0, turned[1], turned[0])
    late_weight, first, second = lax.optimization_barrier((in_weight, first, second))
    weight = lax.all_gather(late_weight[1:], "ctx")
    query_weight = lax.all_gather(late_weight[:1], "ctx")
    out_west = plane_gather(first, x_pairs, y_pairs)
    out_south = plane_gather(second, y_pairs, x_pairs)

    filt = split_taps(medium_filter)
    upper = medium(qkv_first, 256, 1, qkv_first, 1, short_first, filt, 2)
    upper = medium(qkv_first, 256, 1, qkv_first, 1, short_first, filt, 2, 2, (upper,))
    upper_pieces = near_gather(upper)
    lower = medium(rim, HALO, 0, qkv_first, 0, short_first, filt, 4)
    lower_pieces = near_gather(lower)
    hidden_upper, send_upper = mix(
        place, upper_pieces, out_west, out_south, residual_in, norm_gain, 1
    )
    send_upper = token_gather(send_upper)
    hidden_lower, send_lower = mix(
        place, lower_pieces, out_west, out_south, residual_in, norm_gain, 0
    )
    send_lower = token_gather(send_lower)
    hidden = jnp.concatenate([hidden_lower, hidden_upper], axis=0)
    kv_upper = project(place, send_upper, weight, 0, 2)
    edge = lax.ppermute(kv_upper[:, ROWS - 16 :], "ctx", ahead)
    kv_lower = project(place, send_lower, weight, 0, 2)
    u, starts, end = modal_scan(edge, kv_lower, kv_upper, short_second, rates)
    log_decay = -rates * length

    def decay(k):
        return jnp.exp(log_decay * k.astype(jnp.float32))

    along = ring(end, "ctx", x_pairs)
    row = jnp.zeros_like(rates)
    enter = jnp.zeros_like(rates)
    for d, e in enumerate(along):
        at = (x + d) % 4
        wide = e.astype(jnp.float32)
        row = row + decay(3 - at) * wide
        enter = enter + jnp.where(at < x, decay(jnp.maximum(x - 1 - at, 0)), 0.0) * wide
    row = row.astype(jnp.bfloat16)
    up = ring(row, "ctx", y_pairs)
    for d in (1, 2, 3):
        e = up[d]
        at = (y + d) % 4
        enter = enter + jnp.where(
            at < y, decay(x + 4 * jnp.maximum(y - 1 - at, 0)), 0.0
        ) * e.astype(jnp.float32)
    q_upper = project(place, send_upper, query_weight, 0, 1)
    edge = lax.ppermute(q_upper[:, ROWS - 16 :], "ctx", ahead)
    q_lower = project(place, send_lower, query_weight, 0, 1)
    mixed = modal_finish(
        edge, q_lower, q_upper, short_second, rates, residues, skip_gain, u, starts, enter
    )
    return (hidden, mixed)


def solution(mesh):
    placed = (
        P(None, "ctx", "tp"),
        P(None, None, "tp"),
        P("tp", None),
        P("tp", "ctx"),
        P("ctx", "tp"),
        P("tp"),
        P(None, "ctx", "tp"),
        P(None, None, "tp"),
        P(None, "tp"),
        P(None, "tp"),
        P("tp"),
    )
    return jax.shard_map(
        on_device,
        mesh=mesh,
        in_specs=placed,
        out_specs=(P("ctx", "tp"), P("ctx", "tp")),
        check_vma=False,
    )
```
